32 devices in a mesh: role: 4 (over y, x), dom: 8 (over z, core).
Axes of the slice: x: 2, y: 2, z: 4, core: 2. Of those that a mesh axis runs over, the one named last changes fastest.
Arguments:
- node_feats: bfloat16 [4096, 512], P(('role', 'dom')), may hold values from -6 to 6
- hub_feats: bfloat16 [128, 512], P(('role', 'dom')), may hold values from -6 to 6
- weight: bfloat16 [1024, 512], replicated, may hold values from -0.1875 to 0.1875
- edge_src: int32 [32, 1024], P(('role', 'dom')), may hold values from 0 to 287, as said below
- edge_dst: int32 [32, 1024], P(('role', 'dom')), may hold values from 0 to 127, as said below
- bound_rows: int32 [32, 16], P(('role', 'dom')), may hold values from 0 to 127
- hub_edge_src: int32 [32, 128], P(('role', 'dom')), may hold values from 0 to 127
- hub_edge_slot: int32 [32, 128], P(('role', 'dom')), may hold values from 0 to 63, as said below
- slot_hub: int32 [32, 64], P(('role', 'dom')), may hold values from 0 to 3, as said below
Outputs:
- node_out: bfloat16 [4096, 512], P(('role', 'dom'))
- hub_out: bfloat16 [128, 512], P(('role', 'dom'))
The draws below stay inside these ranges and needn't reach their ends.
Inputs may be any that keep to these rules, and one draw needn't show every extreme that they name: `edge_src`: row indices into the source table of the device: its own nodes, then 16 rows of the device before it along dom, then 16 of the device after it, then the 128 hubs. `edge_dst`: each node of a device is the destination of at least one of the device's edges. `hub_edge_slot`: every slot of a device receives at least one of its hub edges; slot s belongs to the owner numbered s // 2. `slot_hub`: every hub of every owner is fed by at least one slot of some device.
All inputs are finite; a program needn't handle non-finite values.
Results may differ from the reference program's by a relative error of at most 0.0027.
Values may be sent and summed in bfloat16 or wider, within the bound.
A program may use at most 64 MiB of HBM per device.

```python
import jax
import jax.numpy as jnp
from jax import lax

D = 512
NODE_DEV = 128
HUB_DEV = 4
CAP = 2
E_DEV = 1024
BOUND = 16
NODES = 4096
HUBS = 128
SLOTS = 64
HUB_EDGES = 128
N_ROLE = 4
N_DOM = 8
DEVICES = 32


def covering_list(key, length, total):
    first_key, rest_key = jax.random.split(key)
    devices = N_ROLE * N_DOM
    first_pass = jax.vmap(lambda subkey: jax.random.permutation(subkey, length))(jax.random.split(first_key, devices))
    remaining = jax.random.randint(rest_key, (devices, total - length), 0, length)
    return jnp.concatenate([first_pass.astype(jnp.int32), remaining.astype(jnp.int32)], axis=1)


def draw_edge_src(key, part):
    devices = N_ROLE * N_DOM
    category_key, local_key, side_key, hub_key = jax.random.split(jax.random.fold_in(key, 11), 4)
    shape = (devices, E_DEV)
    category = jax.random.randint(category_key, shape, 0, 10)
    local_pick = jax.random.randint(local_key, shape, 0, NODE_DEV)
    side_pick = jax.random.randint(side_key, shape, 0, 2 * BOUND)
    hub_pick = jax.random.randint(hub_key, shape, 0, HUBS)
    chosen = jnp.where(category < 7, local_pick, jnp.where(category < 9, NODE_DEV + side_pick, NODE_DEV + 2 * BOUND + hub_pick))
    return chosen.astype(jnp.int32)


def draw_edge_dst(key, part):
    return covering_list(jax.random.fold_in(key, 23), NODE_DEV, E_DEV)


def draw_hub_edge_slot(key, part):
    return covering_list(jax.random.fold_in(key, 37), SLOTS, HUB_EDGES)


def draw_slot_hub(key, part):
    devices = N_ROLE * N_DOM
    random_key, order_key = jax.random.split(jax.random.fold_in(key, 41))
    random_hub = jax.random.randint(random_key, (devices, SLOTS), 0, HUB_DEV)
    orders = jax.vmap(lambda subkey: jax.random.permutation(subkey, devices))(jax.random.split(order_key, devices))
    source_rank = jnp.argsort(orders, axis=1, stable=True).astype(jnp.int32)
    covering = source_rank.T[:, :, None] * CAP + jnp.arange(CAP, dtype=jnp.int32)[None, None, :]
    covering = covering.reshape(devices, SLOTS)
    return jnp.where(covering < HUB_DEV, covering, random_hub).astype(jnp.int32)


def plant(values, rng, least, largest):
    longest = values.shape.index(max(values.shape))
    spots = []
    for shift in (0, 1):
        where = [jax.random.randint(jax.random.fold_in(rng, axis), (), 0, length) for axis, length in enumerate(values.shape)]
        where[longest] = (where[longest] + shift) % values.shape[longest]
        spots.append(tuple(where))
    return values.at[spots[0]].set(least).at[spots[1]].set(largest)


def level_of(key, extent, pieces, least, high):
    def one(position, shards_of):
        heights = jax.random.uniform(jax.random.fold_in(jax.random.fold_in(key, 6), position), (shards_of,), jnp.float32, least / len(pieces), high / len(pieces))
        return jnp.repeat(jnp.exp(heights), extent[position] // shards_of).reshape((-1,) + (1,) * (len(extent) - position - 1))

    factor_of = one(*pieces[0])
    for cut in pieces[1:]:
        factor_of = factor_of * one(*cut)
    return factor_of


def scatter_about(stream_key, extent, scale, bound, shards=(), held_as=jnp.bfloat16):
    result = jax.random.normal(stream_key, extent, jnp.float32) * scale
    if len(shards) > 0:
        result = level_of(stream_key, extent, shards, -0.22, 0.18) * result
    return jnp.clip(result, min=-bound, max=bound).astype(held_as)


def setup_inputs(seed: int = 0) -> dict:
    seeds = jax.random.split(jax.random.key(seed), 10)
    return {
        "node_feats": scatter_about(seeds[0], (NODES, D), 1.0, 6.0, ((0, 32),)),
        "hub_feats": scatter_about(seeds[1], (HUBS, D), 1.0, 6.0, ((0, 32),)),
        "weight": scatter_about(seeds[2], (2 * D, D), (2 * D) ** -0.5, 0.1875),
        "edge_src": draw_edge_src(jax.random.fold_in(seeds[9], 71), 0),
        "edge_dst": draw_edge_dst(jax.random.fold_in(seeds[9], 71), 0),
        "bound_rows": plant(jax.random.randint(seeds[5], (DEVICES, BOUND), 0, NODE_DEV), jax.random.fold_in(seeds[5], 1), 0, NODE_DEV - 1).astype(jnp.int32),
        "hub_edge_src": plant(jax.random.randint(seeds[6], (DEVICES, HUB_EDGES), 0, NODE_DEV), jax.random.fold_in(seeds[6], 1), 0, NODE_DEV - 1).astype(jnp.int32),
        "hub_edge_slot": draw_hub_edge_slot(jax.random.fold_in(seeds[9], 71), 0),
        "slot_hub": draw_slot_hub(jax.random.fold_in(seeds[9], 71), 0),
    }


epsilon = 1e-06

def sage_update(self_rows, mean_rows, weight):
    joined = jnp.concatenate([self_rows, mean_rows], axis=1)
    linear = jnp.dot(joined, weight, preferred_element_type=jnp.float32)
    rectified = jnp.maximum(linear, jnp.float32(0.0))
    inverse_norm = lax.rsqrt(lax.optimization_barrier(jnp.mean(rectified * rectified, axis=1, keepdims=True)) + epsilon)
    return (rectified * inverse_norm).astype(jnp.bfloat16)

def reference(node_feats, hub_feats, weight, edge_src, edge_dst, bound_rows, hub_edge_src, hub_edge_slot, slot_hub):
    devices = N_ROLE * N_DOM
    local_rows = node_feats.reshape(devices, NODE_DEV, D)
    exports = jax.vmap(lambda device_rows, picks: device_rows[picks])(local_rows, bound_rows)
    exports = exports.reshape(N_ROLE, N_DOM, BOUND, D)
    before_rows = jnp.roll(exports, 1, axis=1).reshape(devices, BOUND, D)
    after_rows = jnp.roll(exports, -1, axis=1).reshape(devices, BOUND, D)

    def one_device(operands):
        device_rows, before_part, after_part, sources, targets = operands
        source_table = jnp.concatenate([device_rows, before_part, after_part, hub_feats], axis=0)
        picked = source_table[sources].astype(jnp.float32)
        node_sum = jax.ops.segment_sum(picked, targets, num_segments=NODE_DEV)
        node_degree = jax.ops.segment_sum(jnp.ones(sources.shape, jnp.float32), targets, num_segments=NODE_DEV)
        node_mean = (node_sum / node_degree[:, None]).astype(jnp.bfloat16)
        return sage_update(device_rows, node_mean, weight)
    node_out = lax.map(one_device, (local_rows, before_rows, after_rows, edge_src, edge_dst))
    node_out = node_out.reshape(devices * NODE_DEV, D)

    def add_source(sums, operands):
        hub_sum, hub_degree = sums
        device_rows, sources, slot_ids, slot_table = operands
        hub_ids = slot_ids // CAP * HUB_DEV + slot_table[slot_ids]
        picked = device_rows[sources].astype(jnp.float32)
        hub_sum = hub_sum.at[hub_ids].add(picked)
        hub_degree = hub_degree.at[hub_ids].add(jnp.float32(1.0))
        return ((hub_sum, hub_degree), None)
    initial = (jnp.zeros((HUBS, D), jnp.float32), jnp.zeros((HUBS,), jnp.float32))
    (hub_sum, hub_degree), unused = lax.scan(add_source, initial, (local_rows, hub_edge_src, hub_edge_slot, slot_hub))
    hub_mean = (hub_sum / hub_degree[:, None]).astype(jnp.bfloat16)
    hub_out = sage_update(hub_feats, hub_mean, weight)
    return (node_out, hub_out)
```

```python
import functools

import jax
import jax.numpy as jnp
from jax import lax
from jax.experimental import pallas as pl
from jax.experimental.pallas import tpu as pltpu
from jax.sharding import PartitionSpec as P

epsilon = 1e-06
MESH = pl.DeviceIdType.MESH
F32 = jnp.float32
BF16 = jnp.bfloat16
LANES = 128


def dot(a, b):
    return lax.dot_general(a, b, (((1,), (0,)), ((), ())), preferred_element_type=F32)


def dot_t(a, b):
    return lax.dot_general(a, b, (((1,), (1,)), ((), ())), preferred_element_type=F32)


def rows_equal(count, row):
    ids = lax.broadcasted_iota(jnp.int32, (count, row.shape[1]), 0)
    return jnp.where(ids == row, 1.0, 0.0).astype(BF16)


def split(counts):
    high = jnp.floor(counts * (1.0 / 256.0)) * 256.0
    return (counts - high).astype(BF16), high.astype(BF16)


def weighted(counts, table, most):
    if most <= 256:
        return dot(counts.astype(BF16), table)
    low, high = split(counts)
    return dot(low, table) + dot(high, table)


def normalised(linear):
    rectified = jnp.maximum(linear, 0.0)
    scale = lax.rsqrt(jnp.mean(rectified * rectified, axis=1, keepdims=True) + epsilon)
    return (rectified * scale).astype(BF16)


def kernel(
    roles,
    doms,
    node_ref,
    hub_ref,
    weight_hbm,
    edge_src_ref,
    edge_dst_ref,
    bound_ref,
    hub_src_ref,
    hub_slot_ref,
    slot_hub_ref,
    node_out_ref,
    hub_out_ref,
    weight_ref,
    table,
    exports,
    bounds,
    part_out,
    part_in,
    owner_out,
    owner_in,
    weight_sem,
    bound_send,
    bound_recv,
    hub_send_dom,
    hub_recv_dom,
    hub_send_role,
    hub_recv_role,
    part_send,
    part_recv,
    owner_send,
    owner_recv,
):
    r = lax.axis_index("role")
    d = lax.axis_index("dom")
    barrier = pltpu.get_barrier_semaphore()
    for o in range(1, doms):
        pl.semaphore_signal(barrier, inc=1, device_id=(r, (d + o) % doms), device_id_type=MESH)
    for o in range(1, roles):
        pl.semaphore_signal(barrier, inc=1, device_id=((r + o) % roles, d), device_id_type=MESH)
    weight_copy = pltpu.make_async_copy(weight_hbm, weight_ref, weight_sem)
    weight_copy.start()

    nodes, width = node_ref.shape
    hub_local = hub_ref.shape[0]
    devices = roles * doms
    hubs = devices * hub_local
    bound = bound_ref.shape[1]
    edges = edge_src_ref.shape[1]
    hub_edges = hub_src_ref.shape[1]
    slots = slot_hub_ref.shape[1]
    per_owner = slots // devices
    node = node_ref[...]

    def copy(src, dst, send, recv, to_role, to_dom):
        return pltpu.make_async_remote_copy(
            src_ref=src, dst_ref=dst, send_sem=send, recv_sem=recv,
            device_id=(to_role, to_dom), device_id_type=MESH,
        )

    table[r, d] = hub_ref[...]
    eye = lax.broadcasted_iota(jnp.int32, (bound, bound), 0) == lax.broadcasted_iota(
        jnp.int32, (bound, bound), 1
    )
    column = jnp.sum(jnp.where(eye, bound_ref[...].astype(F32), 0.0), axis=1, keepdims=True)
    lane = lax.broadcasted_iota(jnp.int32, (bound, nodes), 1).astype(F32)
    pick = jnp.where(lane == column, 1.0, 0.0).astype(BF16)
    exports[...] = dot(pick, node).astype(BF16)

    slot = hub_slot_ref[...]
    slot_onehot = rows_equal(slots, slot)
    slot_hubs = jnp.broadcast_to(slot_hub_ref[...].astype(F32), (8, slots)).astype(BF16)
    hub_number = dot(slot_hubs, slot_onehot)[0:1, :].astype(jnp.int32)
    owner_onehot = rows_equal(hubs, (slot // per_owner) * hub_local + hub_number)
    hub_counts = dot_t(owner_onehot, rows_equal(nodes, hub_src_ref[...]))
    hub_part = weighted(hub_counts, node, hub_edges)
    degree = jnp.sum(hub_counts, axis=1, keepdims=True)
    degree_high = jnp.floor(degree * (1.0 / 256.0)) * 256.0
    lanes = lax.broadcasted_iota(jnp.int32, (hubs, LANES), 1)
    extra = jnp.where(lanes == 0, degree - degree_high, jnp.where(lanes == 1, degree_high, 0.0))
    group = doms * hub_local
    part_out[:, :, 0:width] = hub_part.astype(BF16).reshape(roles, group, width)
    part_out[:, :, width:] = extra.astype(BF16).reshape(roles, group, LANES)

    pl.semaphore_wait(barrier, doms - 1 + roles - 1)

    hub_dom = []
    for o in range(1, doms):
        c = copy(hub_ref, table.at[r, d], hub_send_dom.at[o - 1], hub_recv_dom.at[o - 1], r, (d + o) % doms)
        c.start()
        hub_dom.append(c)
    parts = []
    for o in range(1, roles):
        to = (r + o) % roles
        c = copy(part_out.at[to], part_in.at[o - 1], part_send.at[o - 1], part_recv.at[o - 1], to, d)
        c.start()
        parts.append(c)
    sides = []
    for side, step in ((0, 1), (1, doms - 1)):
        c = copy(exports, bounds.at[side], bound_send.at[side], bound_recv.at[side], r, (d + step) % doms)
        c.start()
        sides.append(c)

    source = edge_src_ref[...]
    target_onehot = rows_equal(nodes, edge_dst_ref[...])
    counts_local = dot_t(target_onehot, rows_equal(nodes, source))
    counts_hub = dot_t(target_onehot, rows_equal(hubs, source - (nodes + 2 * bound)))

    for o in range(1, doms):
        copy(
            hub_ref, table.at[r, (d + doms - o) % doms], hub_send_dom.at[o - 1], hub_recv_dom.at[o - 1], r, d
        ).wait_recv()
    hub_role = []
    for o in range(1, roles):
        c = copy(
            table.at[r], table.at[r], hub_send_role.at[o - 1], hub_recv_role.at[o - 1], (r + o) % roles, d
        )
        c.start()
        hub_role.append(c)

    for c in parts:
        c.wait_recv()
    owner_part = part_out[r].astype(F32)
    for o in range(1, roles):
        owner_part = owner_part + part_in[o - 1].astype(F32)
    for j in range(doms):
        owner_out[j] = owner_part[j * hub_local : (j + 1) * hub_local]
    owners = []
    counts_bound = dot_t(target_onehot, rows_equal(2 * bound, source - nodes))
    for o in range(1, doms):
        to = (d + o) % doms
        c = copy(owner_out.at[to], owner_in.at[o - 1], owner_send.at[o - 1], owner_recv.at[o - 1], r, to)
        c.start()
        owners.append(c)

    node_degree = (
        jnp.sum(counts_local, axis=1, keepdims=True)
        + jnp.sum(counts_hub, axis=1, keepdims=True)
        + jnp.sum(counts_bound, axis=1, keepdims=True)
    )
    node_sum = weighted(counts_local, node, edges)
    weight_copy.wait()
    node_linear = dot(node, weight_ref[0:width])
    hub_linear = dot(hub_ref[...], weight_ref[0:width])
    for c in sides:
        c.wait_recv()
    node_sum = node_sum + weighted(counts_bound, bounds[...].reshape(2 * bound, width), edges)

    for o in range(1, roles):
        source_role = (r + roles - o) % roles
        copy(
            table.at[r], table.at[source_role], hub_send_role.at[o - 1], hub_recv_role.at[o - 1], r, d
        ).wait_recv()
    hub_table = table[...].astype(F32).reshape(hubs, width).astype(BF16)
    node_sum = node_sum + weighted(counts_hub, hub_table, edges)
    node_mean = (node_sum / node_degree).astype(BF16)
    node_out_ref[...] = normalised(node_linear + dot(node_mean, weight_ref[width:]))

    for c in owners:
        c.wait_recv()
    owner_sum = owner_out[d]
    for o in range(1, doms):
        owner_sum = owner_sum + owner_in[o - 1]
    hub_degree = jnp.sum(owner_sum[:, width:], axis=1, keepdims=True)
    hub_mean = (owner_sum[:, 0:width] / hub_degree).astype(BF16)
    hub_out_ref[...] = normalised(hub_linear + dot(hub_mean, weight_ref[width:]))

    for c in hub_dom + parts + sides + hub_role + owners:
        c.wait_send()


def solution(mesh):
    roles, doms = mesh.shape["role"], mesh.shape["dom"]

    def on_device(node, hub, weight, *lists):
        nodes, width = node.shape
        hub_local = hub.shape[0]
        bound = lists[2].shape[1]
        vmem = pl.BlockSpec(memory_space=pltpu.VMEM)
        dma = pltpu.SemaphoreType.DMA
        return pl.pallas_call(
            functools.partial(kernel, roles, doms),
            out_shape=(
                jax.ShapeDtypeStruct(node.shape, BF16),
                jax.ShapeDtypeStruct(hub.shape, BF16),
            ),
            in_specs=[vmem, vmem, pl.BlockSpec(memory_space=pl.ANY)] + [vmem] * 6,
            out_specs=(vmem, vmem),
            scratch_shapes=[
                pltpu.VMEM(weight.shape, BF16),
                pltpu.VMEM((roles, doms, hub_local, width), BF16),
                pltpu.VMEM((bound, width), BF16),
                pltpu.VMEM((2, bound, width), BF16),
                pltpu.VMEM((roles, doms * hub_local, width + LANES), BF16),
                pltpu.VMEM((roles - 1, doms * hub_local, width + LANES), BF16),
                pltpu.VMEM((doms, hub_local, width + LANES), F32),
                pltpu.VMEM((doms - 1, hub_local, width + LANES), F32),
                dma,
                dma((2,)),
                dma((2,)),
                dma((doms - 1,)),
                dma((doms - 1,)),
                dma((roles - 1,)),
                dma((roles - 1,)),
                dma((roles - 1,)),
                dma((roles - 1,)),
                dma((doms - 1,)),
                dma((doms - 1,)),
            ],
            compiler_params=pltpu.CompilerParams(collective_id=0, has_side_effects=True),
        )(node, hub, weight, *lists)

    split_rows = P(("role", "dom"), None)
    return jax.shard_map(
        on_device,
        mesh=mesh,
        in_specs=(split_rows, split_rows, P()) + (split_rows,) * 6,
        out_specs=(split_rows, split_rows),
        check_vma=False,
    )
```

```python
import functools

import jax
import jax.numpy as jnp
from jax import lax
from jax.experimental import pallas as pl
from jax.experimental.pallas import tpu as pltpu
from jax.sharding import PartitionSpec as P

epsilon = 1e-06
MESH = pl.DeviceIdType.MESH
F32 = jnp.float32
BF16 = jnp.bfloat16
LANES = 128


def dot(a, b):
    return lax.dot_general(a, b, (((1,), (0,)), ((), ())), preferred_element_type=F32)


def dot_t(a, b):
    return lax.dot_general(a, b, (((1,), (1,)), ((), ())), preferred_element_type=F32)


def rows_equal(count, row):
    ids = lax.broadcasted_iota(jnp.int32, (count, row.shape[1]), 0)
    return jnp.where(ids == row, 1.0, 0.0).astype(BF16)


def split(counts):
    high = jnp.floor(counts * (1.0 / 256.0)) * 256.0
    return (counts - high).astype(BF16), high.astype(BF16)


def weighted(counts, table, most):
    if most <= 256:
        return dot(counts.astype(BF16), table)
    low, high = split(counts)
    return dot(low, table) + dot(high, table)


def normalised(linear):
    rectified = jnp.maximum(linear, 0.0)
    scale = lax.rsqrt(jnp.mean(rectified * rectified, axis=1, keepdims=True) + epsilon)
    return (rectified * scale).astype(BF16)


def kernel(
    roles,
    doms,
    *refs,
):
    inputs, refs = refs[:9], refs[9:]
    (node_out_ref, hub_out_ref), refs = refs[:2], refs[2:]
    held, refs = refs[:9], refs[9:]
    body(roles, doms, inputs, held, node_out_ref, hub_out_ref, *refs)


def body(
    roles,
    doms,
    inputs,
    held,
    node_out_ref,
    hub_out_ref,
    load_sems,
    table,
    exports,
    bounds,
    part_out,
    part_in,
    owner_out,
    owner_in,
    bound_send,
    bound_recv,
    hub_send_dom,
    hub_recv_dom,
    hub_send_role,
    hub_recv_role,
    part_send,
    part_recv,
    owner_send,
    owner_recv,
):
    r = lax.axis_index("role")
    d = lax.axis_index("dom")
    barrier = pltpu.get_barrier_semaphore()
    for o in range(1, doms):
        pl.semaphore_signal(barrier, inc=1, device_id=(r, (d + o) % doms), device_id_type=MESH)
    for o in range(1, roles):
        pl.semaphore_signal(barrier, inc=1, device_id=((r + o) % roles, d), device_id_type=MESH)
    loads = [pltpu.make_async_copy(inputs[i], held[i], load_sems.at[i]) for i in range(9)]
    for i in (7, 8, 6, 0, 5, 1, 3, 4, 2):
        loads[i].start()
    node_ref, hub_ref, weight_ref, edge_src_ref, edge_dst_ref = held[:5]
    bound_ref, hub_src_ref, hub_slot_ref, slot_hub_ref = held[5:]

    nodes, width = node_ref.shape
    hub_local = hub_ref.shape[0]
    devices = roles * doms
    hubs = devices * hub_local
    bound = bound_ref.shape[1]
    edges = edge_src_ref.shape[1]
    hub_edges = hub_src_ref.shape[1]
    slots = slot_hub_ref.shape[1]
    per_owner = slots // devices

    def copy(src, dst, send, recv, to_role, to_dom):
        return pltpu.make_async_remote_copy(
            src_ref=src, dst_ref=dst, send_sem=send, recv_sem=recv,
            device_id=(to_role, to_dom), device_id_type=MESH,
        )

    for i in (7, 8, 6):
        loads[i].wait()
    slot = hub_slot_ref[...]
    slot_onehot = rows_equal(slots, slot)
    slot_hubs = jnp.broadcast_to(slot_hub_ref[...].astype(F32), (8, slots)).astype(BF16)
    hub_number = dot(slot_hubs, slot_onehot)[0:1, :].astype(jnp.int32)
    owner_onehot = rows_equal(hubs, (slot // per_owner) * hub_local + hub_number)
    hub_counts = dot_t(owner_onehot, rows_equal(nodes, hub_src_ref[...]))
    for i in (0, 5, 1):
        loads[i].wait()
    node = node_ref[...]
    table[r, d] = hub_ref[...]
    eye = lax.broadcasted_iota(jnp.int32, (bound, bound), 0) == lax.broadcasted_iota(
        jnp.int32, (bound, bound), 1
    )
    column = jnp.sum(jnp.where(eye, bound_ref[...].astype(F32), 0.0), axis=1, keepdims=True)
    lane = lax.broadcasted_iota(jnp.int32, (bound, nodes), 1).astype(F32)
    pick = jnp.where(lane == column, 1.0, 0.0).astype(BF16)
    exports[...] = dot(pick, node).astype(BF16)

    hub_part = weighted(hub_counts, node, hub_edges)
    degree = jnp.sum(hub_counts, axis=1, keepdims=True)
    degree_high = jnp.floor(degree * (1.0 / 256.0)) * 256.0
    lanes = lax.broadcasted_iota(jnp.int32, (hubs, LANES), 1)
    extra = jnp.where(lanes == 0, degree - degree_high, jnp.where(lanes == 1, degree_high, 0.0))
    group = doms * hub_local
    part_out[:, :, 0:width] = hub_part.astype(BF16).reshape(roles, group, width)
    part_out[:, :, width:] = extra.astype(BF16).reshape(roles, group, LANES)

    pl.semaphore_wait(barrier, doms - 1 + roles - 1)

    hub_dom = []
    for o in range(1, doms):
        c = copy(hub_ref, table.at[r, d], hub_send_dom.at[o - 1], hub_recv_dom.at[o - 1], r, (d + o) % doms)
        c.start()
        hub_dom.append(c)
    parts = []
    for o in range(1, roles):
        to = (r + o) % roles
        c = copy(part_out.at[to], part_in.at[o - 1], part_send.at[o - 1], part_recv.at[o - 1], to, d)
        c.start()
        parts.append(c)
    sides = []
    for side, step in ((0, 1), (1, doms - 1)):
        c = copy(exports, bounds.at[side], bound_send.at[side], bound_recv.at[side], r, (d + step) % doms)
        c.start()
        sides.append(c)

    loads[3].wait()
    loads[4].wait()
    source = edge_src_ref[...]
    target_onehot = rows_equal(nodes, edge_dst_ref[...])
    counts_local = dot_t(target_onehot, rows_equal(nodes, source))
    counts_hub = dot_t(target_onehot, rows_equal(hubs, source - (nodes + 2 * bound)))

    for o in range(1, doms):
        copy(
            hub_ref, table.at[r, (d + doms - o) % doms], hub_send_dom.at[o - 1], hub_recv_dom.at[o - 1], r, d
        ).wait_recv()
    hub_role = []
    for o in range(1, roles):
        c = copy(
            table.at[r], table.at[r], hub_send_role.at[o - 1], hub_recv_role.at[o - 1], (r + o) % roles, d
        )
        c.start()
        hub_role.append(c)

    for c in parts:
        c.wait_recv()
    owner_part = part_out[r].astype(F32)
    for o in range(1, roles):
        owner_part = owner_part + part_in[o - 1].astype(F32)
    for j in range(doms):
        owner_out[j] = owner_part[j * hub_local : (j + 1) * hub_local]
    owners = []
    counts_bound = dot_t(target_onehot, rows_equal(2 * bound, source - nodes))
    for o in range(1, doms):
        to = (d + o) % doms
        c = copy(owner_out.at[to], owner_in.at[o - 1], owner_send.at[o - 1], owner_recv.at[o - 1], r, to)
        c.start()
        owners.append(c)

    node_degree = (
        jnp.sum(counts_local, axis=1, keepdims=True)
        + jnp.sum(counts_hub, axis=1, keepdims=True)
        + jnp.sum(counts_bound, axis=1, keepdims=True)
    )
    node_sum = weighted(counts_local, node, edges)
    loads[2].wait()
    node_linear = dot(node, weight_ref[0:width])
    hub_linear = dot(hub_ref[...], weight_ref[0:width])
    for c in sides:
        c.wait_recv()
    node_sum = node_sum + weighted(counts_bound, bounds[...].reshape(2 * bound, width), edges)

    for o in range(1, roles):
        source_role = (r + roles - o) % roles
        copy(
            table.at[r], table.at[source_role], hub_send_role.at[o - 1], hub_recv_role.at[o - 1], r, d
        ).wait_recv()
    hub_table = table[...].astype(F32).reshape(hubs, width).astype(BF16)
    node_sum = node_sum + weighted(counts_hub, hub_table, edges)
    node_mean = (node_sum / node_degree).astype(BF16)
    node_out_ref[...] = normalised(node_linear + dot(node_mean, weight_ref[width:]))

    for c in owners:
        c.wait_recv()
    owner_sum = owner_out[d]
    for o in range(1, doms):
        owner_sum = owner_sum + owner_in[o - 1]
    hub_degree = jnp.sum(owner_sum[:, width:], axis=1, keepdims=True)
    hub_mean = (owner_sum[:, 0:width] / hub_degree).astype(BF16)
    hub_out_ref[...] = normalised(hub_linear + dot(hub_mean, weight_ref[width:]))

    for c in hub_dom + parts + sides + hub_role + owners:
        c.wait_send()


def hand_over(node_ref, hub_ref, node_out_ref, hub_out_ref, sems):
    copies = [
        pltpu.make_async_copy(node_ref, node_out_ref, sems.at[0]),
        pltpu.make_async_copy(hub_ref, hub_out_ref, sems.at[1]),
    ]
    for c in copies:
        c.start()
    for c in copies:
        c.wait()


def solution(mesh):
    roles, doms = mesh.shape["role"], mesh.shape["dom"]

    def on_device(node, hub, weight, *lists):
        nodes, width = node.shape
        hub_local = hub.shape[0]
        bound = lists[2].shape[1]
        vmem = pl.BlockSpec(memory_space=pltpu.VMEM)
        dma = pltpu.SemaphoreType.DMA
        rows = pl.pallas_call(
            functools.partial(kernel, roles, doms),
            out_shape=(
                pltpu.VMEM(node.shape, BF16),
                pltpu.VMEM(hub.shape, BF16),
            ),
            in_specs=[pl.BlockSpec(memory_space=pl.ANY)] * 9,
            out_specs=(vmem, vmem),
            scratch_shapes=[pltpu.VMEM(x.shape, x.dtype) for x in (node, hub, weight, *lists)]
            + [
                dma((9,)),
                pltpu.VMEM((roles, doms, hub_local, width), BF16),
                pltpu.VMEM((bound, width), BF16),
                pltpu.VMEM((2, bound, width), BF16),
                pltpu.VMEM((roles, doms * hub_local, width + LANES), BF16),
                pltpu.VMEM((roles - 1, doms * hub_local, width + LANES), BF16),
                pltpu.VMEM((doms, hub_local, width + LANES), F32),
                pltpu.VMEM((doms - 1, hub_local, width + LANES), F32),
                dma((2,)),
                dma((2,)),
                dma((doms - 1,)),
                dma((doms - 1,)),
                dma((roles - 1,)),
                dma((roles - 1,)),
                dma((roles - 1,)),
                dma((roles - 1,)),
                dma((doms - 1,)),
                dma((doms - 1,)),
            ],
            compiler_params=pltpu.CompilerParams(collective_id=0, has_side_effects=True),
        )(node, hub, weight, *lists)
        return tuple(rows)

    split_rows = P(("role", "dom"), None)
    return jax.shard_map(
        on_device,
        mesh=mesh,
        in_specs=(split_rows, split_rows, P()) + (split_rows,) * 6,
        out_specs=(split_rows, split_rows),
        check_vma=False,
    )
```

```python
import functools

import jax
import jax.numpy as jnp
from jax import lax
from jax.experimental import pallas as pl
from jax.experimental.pallas import tpu as pltpu
from jax.sharding import PartitionSpec as P

epsilon = 1e-06
MESH = pl.DeviceIdType.MESH
F32 = jnp.float32
BF16 = jnp.bfloat16
LANES = 128


def dot(a, b):
    return lax.dot_general(a, b, (((1,), (0,)), ((), ())), preferred_element_type=F32)


def dot_t(a, b):
    return lax.dot_general(a, b, (((1,), (1,)), ((), ())), preferred_element_type=F32)


def rows_equal(count, row):
    ids = lax.broadcasted_iota(jnp.int32, (count, row.shape[1]), 0)
    return jnp.where(ids == row, 1.0, 0.0).astype(BF16)


def split(counts):
    high = jnp.floor(counts * (1.0 / 256.0)) * 256.0
    return (counts - high).astype(BF16), high.astype(BF16)


def weighted(counts, table, most):
    if most <= 256:
        return dot(counts.astype(BF16), table)
    low, high = split(counts)
    return dot(low, table) + dot(high, table)


def normalised(linear):
    rectified = jnp.maximum(linear, 0.0)
    scale = lax.rsqrt(jnp.mean(rectified * rectified, axis=1, keepdims=True) + epsilon)
    return (rectified * scale).astype(BF16)


def kernel(
    roles,
    doms,
    *refs,
):
    inputs, refs = refs[:9], refs[9:]
    (node_out_ref, hub_out_ref), refs = refs[:2], refs[2:]
    held, refs = refs[:9], refs[9:]
    body(roles, doms, inputs, held, node_out_ref, hub_out_ref, *refs)


def body(
    roles,
    doms,
    inputs,
    held,
    node_out_ref,
    hub_out_ref,
    load_sems,
    table,
    exports,
    bounds,
    part_out,
    part_in,
    owner_out,
    owner_in,
    bound_send,
    bound_recv,
    hub_send_dom,
    hub_recv_dom,
    hub_send_role,
    hub_recv_role,
    part_send,
    part_recv,
    owner_send,
    owner_recv,
):
    r = lax.axis_index("role")
    d = lax.axis_index("dom")
    barrier = pltpu.get_barrier_semaphore()
    for o in range(1, doms):
        pl.semaphore_signal(barrier, inc=1, device_id=(r, (d + o) % doms), device_id_type=MESH)
    for o in range(1, roles):
        pl.semaphore_signal(barrier, inc=1, device_id=((r + o) % roles, d), device_id_type=MESH)
    loads = [pltpu.make_async_copy(inputs[i], held[i], load_sems.at[i]) for i in range(9)]
    for i in (7, 8, 6, 0, 5, 1, 3, 4, 2):
        loads[i].start()
    node_ref, hub_ref, weight_ref, edge_src_ref, edge_dst_ref = held[:5]
    bound_ref, hub_src_ref, hub_slot_ref, slot_hub_ref = held[5:]

    nodes, width = node_ref.shape
    hub_local = hub_ref.shape[0]
    devices = roles * doms
    hubs = devices * hub_local
    bound = bound_ref.shape[1]
    edges = edge_src_ref.shape[1]
    hub_edges = hub_src_ref.shape[1]
    slots = slot_hub_ref.shape[1]
    per_owner = slots // devices

    def copy(src, dst, send, recv, to_role, to_dom):
        return pltpu.make_async_remote_copy(
            src_ref=src, dst_ref=dst, send_sem=send, recv_sem=recv,
            device_id=(to_role, to_dom), device_id_type=MESH,
        )

    for i in (7, 8, 6):
        loads[i].wait()
    slot = hub_slot_ref[...]
    slot_onehot = rows_equal(slots, slot)
    slot_hubs = jnp.broadcast_to(slot_hub_ref[...].astype(F32), (8, slots)).astype(BF16)
    hub_number = dot(slot_hubs, slot_onehot)[0:1, :].astype(jnp.int32)
    owner_onehot = rows_equal(hubs, (slot // per_owner) * hub_local + hub_number)
    hub_counts = dot_t(owner_onehot, rows_equal(nodes, hub_src_ref[...]))
    for i in (0, 5, 1):
        loads[i].wait()
    node = node_ref[...]
    table[r, d] = hub_ref[...]
    eye = lax.broadcasted_iota(jnp.int32, (bound, bound), 0) == lax.broadcasted_iota(
        jnp.int32, (bound, bound), 1
    )
    column = jnp.sum(jnp.where(eye, bound_ref[...].astype(F32), 0.0), axis=1, keepdims=True)
    lane = lax.broadcasted_iota(jnp.int32, (bound, nodes), 1).astype(F32)
    pick = jnp.where(lane == column, 1.0, 0.0).astype(BF16)
    exports[...] = dot(pick, node).astype(BF16)

    hub_part = weighted(hub_counts, node, hub_edges)
    degree = jnp.sum(hub_counts, axis=1, keepdims=True)
    degree_high = jnp.floor(degree * (1.0 / 256.0)) * 256.0
    lanes = lax.broadcasted_iota(jnp.int32, (hubs, LANES), 1)
    extra = jnp.where(lanes == 0, degree - degree_high, jnp.where(lanes == 1, degree_high, 0.0))
    group = doms * hub_local
    part_out[:, :, 0:width] = hub_part.astype(BF16).reshape(roles, group, width)
    part_out[:, :, width:] = extra.astype(BF16).reshape(roles, group, LANES)

    pl.semaphore_wait(barrier, doms - 1 + roles - 1)

    hub_dom = []
    for o in range(1, doms):
        c = copy(hub_ref, table.at[r, d], hub_send_dom.at[o - 1], hub_recv_dom.at[o - 1], r, (d + o) % doms)
        c.start()
        hub_dom.append(c)
    parts = []
    for o in range(1, roles):
        to = (r + o) % roles
        c = copy(part_out.at[to], part_in.at[o - 1], part_send.at[o - 1], part_recv.at[o - 1], to, d)
        c.start()
        parts.append(c)
    sides = []
    for side, step in ((0, 1), (1, doms - 1)):
        c = copy(exports, bounds.at[side], bound_send.at[side], bound_recv.at[side], r, (d + step) % doms)
        c.start()
        sides.append(c)

    loads[3].wait()
    loads[4].wait()
    source = edge_src_ref[...]
    target_onehot = rows_equal(nodes, edge_dst_ref[...])
    counts_local = dot_t(target_onehot, rows_equal(nodes, source))
    counts_hub = dot_t(target_onehot, rows_equal(hubs, source - (nodes + 2 * bound)))

    for o in range(1, doms):
        copy(
            hub_ref, table.at[r, (d + doms - o) % doms], hub_send_dom.at[o - 1], hub_recv_dom.at[o - 1], r, d
        ).wait_recv()
    hub_role = []
    for o in range(1, roles):
        c = copy(
            table.at[r], table.at[r], hub_send_role.at[o - 1], hub_recv_role.at[o - 1], (r + o) % roles, d
        )
        c.start()
        hub_role.append(c)

    for c in parts:
        c.wait_recv()
    owner_part = part_out[r].astype(F32)
    for o in range(1, roles):
        owner_part = owner_part + part_in[o - 1].astype(F32)
    for j in range(doms):
        owner_out[j] = owner_part[j * hub_local : (j + 1) * hub_local]
    owners = []
    counts_bound = dot_t(target_onehot, rows_equal(2 * bound, source - nodes))
    for o in range(1, doms):
        to = (d + o) % doms
        c = copy(owner_out.at[to], owner_in.at[o - 1], owner_send.at[o - 1], owner_recv.at[o - 1], r, to)
        c.start()
        owners.append(c)

    node_degree = (
        jnp.sum(counts_local, axis=1, keepdims=True)
        + jnp.sum(counts_hub, axis=1, keepdims=True)
        + jnp.sum(counts_bound, axis=1, keepdims=True)
    )
    node_sum = weighted(counts_local, node, edges)
    loads[2].wait()
    node_linear = dot(node, weight_ref[0:width])
    hub_linear = dot(hub_ref[...], weight_ref[0:width])
    for c in sides:
        c.wait_recv()
    node_sum = node_sum + weighted(counts_bound, bounds[...].reshape(2 * bound, width), edges)

    for o in range(1, roles):
        source_role = (r + roles - o) % roles
        copy(
            table.at[r], table.at[source_role], hub_send_role.at[o - 1], hub_recv_role.at[o - 1], r, d
        ).wait_recv()
    hub_table = table[...].astype(F32).reshape(hubs, width).astype(BF16)
    node_sum = node_sum + weighted(counts_hub, hub_table, edges)
    node_mean = (node_sum / node_degree).astype(BF16)
    node_out_ref[...] = normalised(node_linear + dot(node_mean, weight_ref[width:]))

    for c in owners:
        c.wait_recv()
    owner_sum = owner_out[d]
    for o in range(1, doms):
        owner_sum = owner_sum + owner_in[o - 1]
    hub_degree = jnp.sum(owner_sum[:, width:], axis=1, keepdims=True)
    hub_mean = (owner_sum[:, 0:width] / hub_degree).astype(BF16)
    hub_out_ref[...] = normalised(hub_linear + dot(hub_mean, weight_ref[width:]))

    for c in hub_dom + parts + sides + hub_role + owners:
        c.wait_send()


def hand_over(node_ref, hub_ref, node_out_ref, hub_out_ref, sems):
    copies = [
        pltpu.make_async_copy(node_ref, node_out_ref, sems.at[0]),
        pltpu.make_async_copy(hub_ref, hub_out_ref, sems.at[1]),
    ]
    for c in copies:
        c.start()
    for c in copies:
        c.wait()


def solution(mesh):
    roles, doms = mesh.shape["role"], mesh.shape["dom"]

    def on_device(node, hub, weight, *lists):
        nodes, width = node.shape
        hub_local = hub.shape[0]
        bound = lists[2].shape[1]
        vmem = pl.BlockSpec(memory_space=pltpu.VMEM)
        dma = pltpu.SemaphoreType.DMA
        rows = pl.pallas_call(
            functools.partial(kernel, roles, doms),
            out_shape=(
                pltpu.VMEM(node.shape, BF16),
                pltpu.VMEM(hub.shape, BF16),
            ),
            in_specs=[pl.BlockSpec(memory_space=pl.ANY)] * 9,
            out_specs=(vmem, vmem),
            scratch_shapes=[pltpu.VMEM(x.shape, x.dtype) for x in (node, hub, weight, *lists)]
            + [
                dma((9,)),
                pltpu.VMEM((roles, doms, hub_local, width), BF16),
                pltpu.VMEM((bound, width), BF16),
                pltpu.VMEM((2, bound, width), BF16),
                pltpu.VMEM((roles, doms * hub_local, width + LANES), BF16),
                pltpu.VMEM((roles - 1, doms * hub_local, width + LANES), BF16),
                pltpu.VMEM((doms, hub_local, width + LANES), F32),
                pltpu.VMEM((doms - 1, hub_local, width + LANES), F32),
                dma((2,)),
                dma((2,)),
                dma((doms - 1,)),
                dma((doms - 1,)),
                dma((roles - 1,)),
                dma((roles - 1,)),
                dma((roles - 1,)),
                dma((roles - 1,)),
                dma((doms - 1,)),
                dma((doms - 1,)),
            ],
            compiler_params=pltpu.CompilerParams(collective_id=0, has_side_effects=True),
        )(node, hub, weight, *lists)
        anywhere = pl.BlockSpec(memory_space=pl.ANY)
        return pl.pallas_call(
            hand_over,
            out_shape=(
                jax.ShapeDtypeStruct(node.shape, BF16),
                jax.ShapeDtypeStruct(hub.shape, BF16),
            ),
            in_specs=[anywhere, anywhere],
            out_specs=(anywhere, anywhere),
            scratch_shapes=[dma((2,))],
        )(*(pltpu.with_memory_space_constraint(x, pltpu.VMEM) for x in rows))

    split_rows = P(("role", "dom"), None)
    return jax.shard_map(
        on_device,
        mesh=mesh,
        in_specs=(split_rows, split_rows, P()) + (split_rows,) * 6,
        out_specs=(split_rows, split_rows),
        check_vma=False,
    )
```

```python
import functools

import jax
import jax.numpy as jnp
from jax import lax
from jax.experimental import pallas as pl
from jax.experimental.pallas import tpu as pltpu
from jax.sharding import PartitionSpec as P

epsilon = 1e-06
MESH = pl.DeviceIdType.MESH
F32 = jnp.float32
BF16 = jnp.bfloat16
LANES = 128


def dot(a, b):
    return lax.dot_general(a, b, (((1,), (0,)), ((), ())), preferred_element_type=F32)


def dot_t(a, b):
    return lax.dot_general(a, b, (((1,), (1,)), ((), ())), preferred_element_type=F32)


def rows_equal(count, row):
    ids = lax.broadcasted_iota(jnp.int32, (count, row.shape[1]), 0)
    return jnp.where(ids == row, 1.0, 0.0).astype(BF16)


def split(counts):
    high = jnp.floor(counts * (1.0 / 256.0)) * 256.0
    return (counts - high).astype(BF16), high.astype(BF16)


def weighted(counts, table, most):
    if most <= 256:
        return dot(counts.astype(BF16), table)
    both = jnp.concatenate(split(counts), axis=1)
    return dot(both, jnp.concatenate([table, table], axis=0))


def normalised(linear):
    rectified = jnp.maximum(linear, 0.0)
    scale = lax.rsqrt(jnp.mean(rectified * rectified, axis=1, keepdims=True) + epsilon)
    return (rectified * scale).astype(BF16)


def kernel(
    roles,
    doms,
    *refs,
):
    inputs, refs = refs[:9], refs[9:]
    (node_out_ref, hub_out_ref), refs = refs[:2], refs[2:]
    held, refs = refs[:9], refs[9:]
    body(roles, doms, inputs, held, node_out_ref, hub_out_ref, *refs)


def body(
    roles,
    doms,
    inputs,
    held,
    node_out_ref,
    hub_out_ref,
    load_sems,
    table,
    exports,
    bounds,
    part_out,
    part_in,
    owner_out,
    owner_in,
    bound_send,
    bound_recv,
    hub_send_dom,
    hub_recv_dom,
    hub_send_role,
    hub_recv_role,
    part_send,
    part_recv,
    owner_send,
    owner_recv,
):
    r = lax.axis_index("role")
    d = lax.axis_index("dom")
    barrier = pltpu.get_barrier_semaphore()
    for o in range(1, doms):
        pl.semaphore_signal(barrier, inc=1, device_id=(r, (d + o) % doms), device_id_type=MESH)
    for o in range(1, roles):
        pl.semaphore_signal(barrier, inc=1, device_id=((r + o) % roles, d), device_id_type=MESH)
    loads = [pltpu.make_async_copy(inputs[i], held[i], load_sems.at[i]) for i in range(9)]
    for i in (7, 8, 6, 0, 5, 1, 3, 4, 2):
        loads[i].start()
    node_ref, hub_ref, weight_ref, edge_src_ref, edge_dst_ref = held[:5]
    bound_ref, hub_src_ref, hub_slot_ref, slot_hub_ref = held[5:]

    nodes, width = node_ref.shape
    hub_local = hub_ref.shape[0]
    devices = roles * doms
    hubs = devices * hub_local
    bound = bound_ref.shape[1]
    edges = edge_src_ref.shape[1]
    hub_edges = hub_src_ref.shape[1]
    slots = slot_hub_ref.shape[1]
    per_owner = slots // devices

    def copy(src, dst, send, recv, to_role, to_dom):
        return pltpu.make_async_remote_copy(
            src_ref=src, dst_ref=dst, send_sem=send, recv_sem=recv,
            device_id=(to_role, to_dom), device_id_type=MESH,
        )

    for i in (7, 8, 6):
        loads[i].wait()
    slot = hub_slot_ref[...]
    slot_onehot = rows_equal(slots, slot)
    slot_hubs = jnp.broadcast_to(slot_hub_ref[...].astype(F32), (8, slots)).astype(BF16)
    hub_number = dot(slot_hubs, slot_onehot)[0:1, :].astype(jnp.int32)
    owner_onehot = rows_equal(hubs, (slot // per_owner) * hub_local + hub_number)
    hub_counts = dot_t(owner_onehot, rows_equal(nodes, hub_src_ref[...]))
    for i in (0, 5, 1):
        loads[i].wait()
    node = node_ref[...]
    table[r, d] = hub_ref[...]
    eye = lax.broadcasted_iota(jnp.int32, (bound, bound), 0) == lax.broadcasted_iota(
        jnp.int32, (bound, bound), 1
    )
    column = jnp.sum(jnp.where(eye, bound_ref[...].astype(F32), 0.0), axis=1, keepdims=True)
    lane = lax.broadcasted_iota(jnp.int32, (bound, nodes), 1).astype(F32)
    pick = jnp.where(lane == column, 1.0, 0.0).astype(BF16)

    hub_part = weighted(hub_counts, node, hub_edges)
    degree = jnp.sum(hub_counts, axis=1, keepdims=True)
    degree_high = jnp.floor(degree * (1.0 / 256.0)) * 256.0
    lanes = lax.broadcasted_iota(jnp.int32, (hubs, LANES), 1)
    extra = jnp.where(lanes == 0, degree - degree_high, jnp.where(lanes == 1, degree_high, 0.0))
    group = doms * hub_local
    part_out[:, :, 0:width] = hub_part.astype(BF16).reshape(roles, group, width)
    part_out[:, :, width:] = extra.astype(BF16).reshape(roles, group, LANES)

    exports[...] = dot(pick, node).astype(BF16)
    pl.semaphore_wait(barrier, doms - 1 + roles - 1)

    hub_dom = []
    for o in range(1, doms):
        c = copy(hub_ref, table.at[r, d], hub_send_dom.at[o - 1], hub_recv_dom.at[o - 1], r, (d + o) % doms)
        c.start()
        hub_dom.append(c)
    parts = []
    for o in range(1, roles):
        to = (r + o) % roles
        c = copy(part_out.at[to], part_in.at[o - 1], part_send.at[o - 1], part_recv.at[o - 1], to, d)
        c.start()
        parts.append(c)
    sides = []
    for side, step in ((0, 1), (1, doms - 1)):
        c = copy(exports, bounds.at[side], bound_send.at[side], bound_recv.at[side], r, (d + step) % doms)
        c.start()
        sides.append(c)

    loads[3].wait()
    loads[4].wait()
    source = edge_src_ref[...]
    target_onehot = rows_equal(nodes, edge_dst_ref[...])
    counts_local = dot_t(target_onehot, rows_equal(nodes, source))
    counts_hub = dot_t(target_onehot, rows_equal(hubs, source - (nodes + 2 * bound)))

    for o in range(1, doms):
        copy(
            hub_ref, table.at[r, (d + doms - o) % doms], hub_send_dom.at[o - 1], hub_recv_dom.at[o - 1], r, d
        ).wait_recv()
    hub_role = []
    for o in range(1, roles):
        c = copy(
            table.at[r], table.at[r], hub_send_role.at[o - 1], hub_recv_role.at[o - 1], (r + o) % roles, d
        )
        c.start()
        hub_role.append(c)

    for c in parts:
        c.wait_recv()
    owner_part = part_out[r].astype(F32)
    for o in range(1, roles):
        owner_part = owner_part + part_in[o - 1].astype(F32)
    for j in range(doms):
        owner_out[j] = owner_part[j * hub_local : (j + 1) * hub_local]
    owners = []
    counts_bound = dot_t(target_onehot, rows_equal(2 * bound, source - nodes))
    for o in range(1, doms):
        to = (d + o) % doms
        c = copy(owner_out.at[to], owner_in.at[o - 1], owner_send.at[o - 1], owner_recv.at[o - 1], r, to)
        c.start()
        owners.append(c)

    node_degree = (
        jnp.sum(counts_local, axis=1, keepdims=True)
        + jnp.sum(counts_hub, axis=1, keepdims=True)
        + jnp.sum(counts_bound, axis=1, keepdims=True)
    )
    node_sum = weighted(counts_local, node, edges)
    loads[2].wait()
    node_linear = dot(node, weight_ref[0:width])
    hub_linear = dot(hub_ref[...], weight_ref[0:width])
    for c in sides:
        c.wait_recv()
    node_sum = node_sum + weighted(counts_bound, bounds[...].reshape(2 * bound, width), edges)

    for o in range(1, roles):
        source_role = (r + roles - o) % roles
        copy(
            table.at[r], table.at[source_role], hub_send_role.at[o - 1], hub_recv_role.at[o - 1], r, d
        ).wait_recv()
    hub_table = table[...].astype(F32).reshape(hubs, width).astype(BF16)
    node_sum = node_sum + weighted(counts_hub, hub_table, edges)
    node_mean = (node_sum / node_degree).astype(BF16)
    node_out_ref[...] = normalised(node_linear + dot(node_mean, weight_ref[width:]))

    for c in owners:
        c.wait_recv()
    owner_sum = owner_out[d]
    for o in range(1, doms):
        owner_sum = owner_sum + owner_in[o - 1]
    hub_degree = jnp.sum(owner_sum[:, width:], axis=1, keepdims=True)
    hub_mean = (owner_sum[:, 0:width] / hub_degree).astype(BF16)
    hub_out_ref[...] = normalised(hub_linear + dot(hub_mean, weight_ref[width:]))

    for c in hub_dom + parts + sides + hub_role + owners:
        c.wait_send()


def hand_over(node_ref, hub_ref, node_out_ref, hub_out_ref, sems):
    copies = [
        pltpu.make_async_copy(node_ref, node_out_ref, sems.at[0]),
        pltpu.make_async_copy(hub_ref, hub_out_ref, sems.at[1]),
    ]
    for c in copies:
        c.start()
    for c in copies:
        c.wait()


def solution(mesh):
    roles, doms = mesh.shape["role"], mesh.shape["dom"]

    def on_device(node, hub, weight, *lists):
        nodes, width = node.shape
        hub_local = hub.shape[0]
        bound = lists[2].shape[1]
        vmem = pl.BlockSpec(memory_space=pltpu.VMEM)
        dma = pltpu.SemaphoreType.DMA
        rows = pl.pallas_call(
            functools.partial(kernel, roles, doms),
            out_shape=(
                pltpu.VMEM(node.shape, BF16),
                pltpu.VMEM(hub.shape, BF16),
            ),
            in_specs=[pl.BlockSpec(memory_space=pl.ANY)] * 9,
            out_specs=(vmem, vmem),
            scratch_shapes=[pltpu.VMEM(x.shape, x.dtype) for x in (node, hub, weight, *lists)]
            + [
                dma((9,)),
                pltpu.VMEM((roles, doms, hub_local, width), BF16),
                pltpu.VMEM((bound, width), BF16),
                pltpu.VMEM((2, bound, width), BF16),
                pltpu.VMEM((roles, doms * hub_local, width + LANES), BF16),
                pltpu.VMEM((roles - 1, doms * hub_local, width + LANES), BF16),
                pltpu.VMEM((doms, hub_local, width + LANES), F32),
                pltpu.VMEM((doms - 1, hub_local, width + LANES), F32),
                dma((2,)),
                dma((2,)),
                dma((doms - 1,)),
                dma((doms - 1,)),
                dma((roles - 1,)),
                dma((roles - 1,)),
                dma((roles - 1,)),
                dma((roles - 1,)),
                dma((doms - 1,)),
                dma((doms - 1,)),
            ],
            compiler_params=pltpu.CompilerParams(collective_id=0, has_side_effects=True),
        )(node, hub, weight, *lists)
        anywhere = pl.BlockSpec(memory_space=pl.ANY)
        return pl.pallas_call(
            hand_over,
            out_shape=(
                jax.ShapeDtypeStruct(node.shape, BF16),
                jax.ShapeDtypeStruct(hub.shape, BF16),
            ),
            in_specs=[anywhere, anywhere],
            out_specs=(anywhere, anywhere),
            scratch_shapes=[dma((2,))],
        )(*(pltpu.with_memory_space_constraint(x, pltpu.VMEM) for x in rows))

    split_rows = P(("role", "dom"), None)
    return jax.shard_map(
        on_device,
        mesh=mesh,
        in_specs=(split_rows, split_rows, P()) + (split_rows,) * 6,
        out_specs=(split_rows, split_rows),
        check_vma=False,
    )
```
